32 devices in a mesh: src: 4 (over y, x), dst: 8 (over z, core).
Axes of the slice: x: 2, y: 2, z: 4, core: 2. Of those that a mesh axis runs over, the one named last changes fastest.
Arguments:
- transition: bfloat16 [32768, 32768], P('src', 'dst'), may hold values from -0.046875 to 0.046875
- emit_cols: bfloat16 [16, 32768], P(None, 'dst'), may hold values from 0.25 to 4
- token_ids: int32 [48, 4], replicated, may hold values from 0 to 15
- alpha_start: bfloat16 [48, 32768], P(None, 'src'), may hold values from -6 to 6
- beta_end: bfloat16 [48, 32768], P(None, 'dst'), may hold values from -6 to 6
- inverse_likelihood: float32 [48], replicated, may hold values from 5 to 80
Outputs:
- counts: float32 [8192, 8192], P('src', 'dst')
The draws below stay inside these ranges and needn't reach their ends.
Inputs may be any that keep to these rules, and one draw needn't show every extreme that they name: `token_ids`: each id selects one of the 16 supplied emission columns.
All inputs are finite; a program needn't handle non-finite values.
Results may differ from the reference program's by a relative error of at most 0.024.
Values may be sent and summed in bfloat16 or wider, within the bound.
No kernel may reach another device: no remote copies, remote signals or barrier semaphores. Data moves between devices by JAX's collectives and lax.ppermute only.
A program may use at most 128 MiB of HBM per device.

```python
import math
import jax
import jax.numpy as jnp
from jax import lax

H = 32768
SEQS = 48
NCOL = 16
N_SRC = 4
N_DST = 8


def place_ends(drawn, rng, least, high):
    place = [jax.random.randint(jax.random.fold_in(rng, axis), (), 0, length) for axis, length in enumerate(drawn.shape)]
    main_axis = drawn.shape.index(max(drawn.shape))
    next_to = place[:main_axis] + [(place[main_axis] + 1) % drawn.shape[main_axis]] + place[main_axis + 1:]
    return drawn.at[tuple(place)].set(least).at[tuple(next_to)].set(high)


def raised(array, own_key, source, target, shards_of, factor):
    def block_of(axis_at):
        return (jnp.arange(array.shape[axis_at]) // (array.shape[axis_at] // shards_of)).reshape((-1,) + (1,) * (array.ndim - 1 - axis_at))

    near = jax.random.permutation(own_key, shards_of)[block_of(target)]
    far = (block_of(target) + shards_of // 2) % shards_of
    return jnp.where((block_of(source) == near) | (block_of(source) == far), factor * array, array)


def level_of(rng, extent, cuts, least, top_value):
    gain, own = 1.0, jax.random.fold_in(rng, 6)
    for dim, blocks in cuts:
        steps = jnp.exp(jax.random.uniform(jax.random.fold_in(own, dim), (blocks,), jnp.float32, least / len(cuts), top_value / len(cuts)))
        gain = gain * jnp.repeat(steps, extent[dim] // blocks).reshape([-1 if axis == dim else 1 for axis in range(len(extent))])
    return gain


def scatter_about(stream_key, shape, deviation, most, split=(), kind=jnp.bfloat16):
    level = level_of(stream_key, shape, split, -0.22, 0.18) if split else 1.0
    result = jax.random.normal(stream_key, shape, jnp.float32) * deviation * level
    return jnp.minimum(jnp.maximum(result, -most), most).astype(kind)


def gaussian_with(own_key, shape, spread, bound, split, heavy, kind=jnp.bfloat16):
    values = spread * jax.random.normal(own_key, shape, jnp.float32)
    if split:
        values = values * level_of(own_key, shape, split, -0.22, 0.18)
    return jnp.clip(raised(values, jax.random.fold_in(own_key, 3), *heavy), -bound, bound).astype(kind)


def setup_inputs(seed: int = 0) -> dict:
    key_of = jax.random.split(jax.random.key(seed), 7)
    return {
        "transition": gaussian_with(key_of[0], (H, H), H ** -0.5, 0.046875, ((0, 4), (1, 8)), (0, 1, 8, 2.0)),
        "emit_cols": jnp.clip(jnp.exp(math.log(4.0) - 2.7725887 * jax.random.uniform(key_of[1], (NCOL, H), jnp.float32) ** level_of(key_of[1], (NCOL, H), ((1, 8),), -0.2, 0.2)), 0.25, 4.0).astype(jnp.bfloat16),
        "token_ids": place_ends(jax.random.randint(key_of[2], (SEQS, 4), 0, NCOL), jax.random.fold_in(key_of[2], 1), 0, NCOL - 1).astype(jnp.int32),
        "alpha_start": scatter_about(key_of[3], (SEQS, H), 1.0, 6.0, ((1, 4),)),
        "beta_end": scatter_about(key_of[4], (SEQS, H), 1.0, 6.0, ((1, 8),)),
        "inverse_likelihood": jnp.clip(jnp.exp(jax.random.uniform(key_of[5], (SEQS,), jnp.float32, math.log(5.0), math.log(80.0))), 5.0, 80.0),
    }


scaling = 0.75


def emitted(emit_cols, token_ids, position):
    return emit_cols[token_ids[:, position]].astype(jnp.float32)


def quarter_cols(values, groups):
    width = values.shape[1] // groups
    shaped = values.reshape(values.shape[0], groups, width)[:, :, : width // 4]
    return shaped.reshape(values.shape[0], groups * (width // 4))


def reference(transition, emit_cols, token_ids, alpha_start, beta_end, inverse_likelihood):
    alphas = [alpha_start]
    for position in range(2):
        image = jnp.dot(alphas[-1], transition, preferred_element_type=jnp.float32)
        alphas.append((scaling * emitted(emit_cols, token_ids, position) * image).astype(jnp.bfloat16))
    carried = (scaling * emitted(emit_cols, token_ids, 3) * beta_end.astype(jnp.float32)).astype(jnp.bfloat16)
    messages = []
    for position in (2, 1):
        beta = lax.dot_general(carried, transition, (((1,), (1,)), ((), ())), preferred_element_type=jnp.float32).astype(jnp.bfloat16)
        carried = (scaling * emitted(emit_cols, token_ids, position) * beta.astype(jnp.float32)).astype(jnp.bfloat16)
        messages.append(carried)
    message_three, message_two = messages[0], messages[1]
    src_tile = H // N_SRC
    dst_tile = H // N_DST
    block = transition.reshape(N_SRC, src_tile, N_DST, dst_tile)[:, : src_tile // 4, :, : dst_tile // 4]
    block = block.reshape(N_SRC * (src_tile // 4), N_DST * (dst_tile // 4))
    weights = inverse_likelihood[:, None]
    outer_sum = jnp.zeros(block.shape, jnp.float32)
    for alpha_rows, message in ((alphas[1], message_two), (alphas[2], message_three)):
        alpha_quarter = quarter_cols(alpha_rows, N_SRC)
        weighted = (weights * quarter_cols(message, N_DST).astype(jnp.float32)).astype(jnp.bfloat16)
        outer_sum = outer_sum + lax.dot_general(alpha_quarter, weighted, (((0,), (0,)), ((), ())), preferred_element_type=jnp.float32)
    return block.astype(jnp.float32) * outer_sum
```

```python
import jax
import jax.numpy as jnp
from jax import lax
from jax.experimental import pallas as pl
from jax.experimental.pallas import tpu as pltpu
from jax.sharding import PartitionSpec as P

scaling = 0.75
F32 = jnp.float32
BF16 = jnp.bfloat16
MIB = 1 << 20


def plain_device(transition, emit_cols, token_ids, alpha_start, beta_end, inverse_likelihood):
    src_tile = transition.shape[0]
    dst_tile = transition.shape[1]
    src_count = lax.axis_size("src")
    dst_count = lax.axis_size("dst")
    tile_ratio = dst_count // src_count
    row_place = lax.axis_index("src")
    col_place = lax.axis_index("dst")
    seq_rows = alpha_start.shape[0]
    column_codes = lax.broadcasted_iota(jnp.int32, (1, emit_cols.shape[0]), 1)

    def emitted(position):
        selector = (token_ids[:, position : position + 1] == column_codes).astype(jnp.bfloat16)
        return jnp.dot(selector, emit_cols, preferred_element_type=jnp.float32)

    def forward(current, position):
        partial_value = jnp.dot(current, transition, preferred_element_type=jnp.float32)
        slice_width = dst_tile // src_count
        shared = lax.psum_scatter(
            partial_value.astype(jnp.bfloat16), "src", scatter_dimension=1, tiled=True
        ).astype(jnp.float32)
        emit_slice = lax.dynamic_slice_in_dim(
            emitted(position), row_place * slice_width, slice_width, 1
        )
        advanced = (scaling * emit_slice * shared).astype(jnp.bfloat16)
        spread = lax.all_gather(advanced, "dst", axis=1, tiled=True)
        shaped = spread.reshape(seq_rows, src_count, tile_ratio, 1, slice_width)
        regrouped = lax.all_to_all(shaped, "src", split_axis=1, concat_axis=3, tiled=True)
        return regrouped.reshape(seq_rows, src_tile)

    def backward(carried, position):
        partial_value = lax.dot_general(
            carried, transition, (((1,), (1,)), ((), ())), preferred_element_type=jnp.float32
        )
        slice_width = src_tile // dst_count
        shared = lax.psum_scatter(partial_value, "dst", scatter_dimension=1, tiled=True).astype(
            jnp.bfloat16
        )
        spread = lax.all_gather(shared, "src", axis=1, tiled=True)
        tiles = spread.reshape(seq_rows, src_count, 1, slice_width)
        outgoing = jnp.broadcast_to(tiles, (seq_rows, src_count, tile_ratio, slice_width)).reshape(
            seq_rows, dst_count, 1, slice_width
        )
        regrouped = lax.all_to_all(outgoing, "dst", split_axis=1, concat_axis=2, tiled=True)
        whole_tile = regrouped.reshape(seq_rows, src_tile)
        own_part = lax.dynamic_slice_in_dim(
            whole_tile, col_place % tile_ratio * dst_tile, dst_tile, 1
        )
        return (scaling * emitted(position) * own_part.astype(jnp.float32)).astype(jnp.bfloat16)

    alpha_one = forward(alpha_start, 0)
    alpha_two = forward(alpha_one, 1)
    message_four = (scaling * emitted(3) * beta_end.astype(jnp.float32)).astype(jnp.bfloat16)
    message_three = backward(message_four, 2)
    message_two = backward(message_three, 1)
    quarter_rows = src_tile // 4
    quarter_width = dst_tile // 4
    weights = inverse_likelihood[:, None]
    outer_sum = jnp.zeros((quarter_rows, quarter_width), jnp.float32)
    for alpha_rows, message in ((alpha_one, message_two), (alpha_two, message_three)):
        weighted = (weights * message[:, :quarter_width].astype(jnp.float32)).astype(jnp.bfloat16)
        outer_sum = outer_sum + lax.dot_general(
            alpha_rows[:, :quarter_rows],
            weighted,
            (((0,), (0,)), ((), ())),
            preferred_element_type=jnp.float32,
        )
    return transition[:quarter_rows, :quarter_width].astype(jnp.float32) * outer_sum


def in_vmem():
    return pl.BlockSpec(memory_space=pltpu.VMEM)


def in_smem():
    return pl.BlockSpec(memory_space=pltpu.SMEM)


def in_place():
    return pl.BlockSpec(memory_space=pl.ANY)


def shaped(*dims, kind=BF16):
    return jax.ShapeDtypeStruct(dims, kind)


def span(index, width):
    return pl.ds(pl.multiple_of(index * width, width), width)


def emitted(token_ref, emit_ref, position, columns):
    codes = lax.broadcasted_iota(jnp.int32, (token_ref.shape[0], emit_ref.shape[0]), 1)
    selector = (token_ref[:, position : position + 1] == codes).astype(BF16)
    return jnp.dot(selector, emit_ref[:, columns], preferred_element_type=F32)


def rows_product(lhs, block):
    return lax.dot_general(lhs, block, (((1,), (1,)), ((), ())), preferred_element_type=F32)


def cost(flops, moved):
    return pl.CostEstimate(flops=int(flops), bytes_accessed=int(moved), transcendentals=0)


def first_pass(place, alpha_start, beta_end, emit_cols, token_ids, transition, groups):
    seqs, src_tile = alpha_start.shape
    dst_tile = beta_end.shape[1]
    rows = min(512, dst_tile)
    steps = dst_tile // rows
    buffers = 4
    width = dst_tile // groups

    def kernel(place_ref, alpha_ref, beta_ref, emit_ref, token_ref, t_ref, *rest):
        slots, (other_ref, message_ref, total, held, sems) = rest[:groups], rest[groups:]
        own, parity = place_ref[0], place_ref[2]

        def fetch(step):
            tile = lax.select(step % 2 == 0, 1 - parity, parity)
            row = pl.multiple_of(tile * dst_tile + step // 2 * rows, rows)
            slot = step % buffers
            return pltpu.make_async_copy(t_ref.at[pl.ds(row, rows), :], held.at[slot], sems.at[slot])

        for step in range(min(buffers - 1, 2 * steps)):
            fetch(jnp.int32(step)).start()
        message = scaling * emitted(token_ref, emit_ref, 3, slice(None)) * beta_ref[...].astype(F32)
        message_ref[...] = message.astype(BF16)
        total[...] = jnp.zeros_like(total)

        def take(step):
            @pl.when(step + buffers - 1 < 2 * steps)
            def _():
                fetch(step + buffers - 1).start()

            fetch(step).wait()
            return held.at[step % buffers]

        def body(pair, carry):
            block = take(2 * pair)
            at = (1 - parity) * steps + pair
            total[...] += jnp.dot(
                alpha_ref[:, span(at, rows)], block[...], preferred_element_type=F32
            )
            other_ref[:, span(pair, rows)] = rows_product(message_ref[...], block[...]).astype(BF16)
            block = take(2 * pair + 1)
            at = parity * steps + pair
            total[...] += jnp.dot(
                alpha_ref[:, span(at, rows)], block[...], preferred_element_type=F32
            )
            return carry

        lax.fori_loop(0, steps, body, 0)
        for r in range(groups):
            slots[r][...] = total[:, span(lax.rem(own + r, groups), width)].astype(BF16)

    return pl.pallas_call(
        kernel,
        name="first_pass",
        in_specs=[in_smem()] + [in_vmem()] * 4 + [in_place()],
        out_specs=[in_vmem()] * (groups + 2),
        out_shape=[shaped(seqs, width)] * groups + [shaped(seqs, dst_tile)] * 2,
        scratch_shapes=[
            pltpu.VMEM((seqs, dst_tile), F32),
            pltpu.VMEM((buffers, rows, dst_tile), BF16),
            pltpu.SemaphoreType.DMA((buffers,)),
        ],
        compiler_params=pltpu.CompilerParams(vmem_limit_bytes=28 * MIB),
        cost_estimate=cost(3 * seqs * src_tile * dst_tile, 2 * src_tile * dst_tile),
    )(place, alpha_start, beta_end, emit_cols, token_ids, transition)


def backward_rows(place, message, transition, part, parts):
    seqs, dst_tile = message.shape
    count = dst_tile // parts
    rows = min(512, count)
    steps = count // rows
    buffers = min(4, steps)

    def kernel(place_ref, message_ref, t_ref, out_ref, held, sems):
        first = place_ref[2] * dst_tile + part * count

        def fetch(step):
            row = pl.multiple_of(first + step * rows, rows)
            slot = step % buffers
            return pltpu.make_async_copy(t_ref.at[pl.ds(row, rows), :], held.at[slot], sems.at[slot])

        for step in range(min(buffers, steps)):
            fetch(jnp.int32(step)).start()

        def body(step, carry):
            fetch(step).wait()
            block = held[step % buffers]
            out_ref[:, span(step, rows)] = rows_product(message_ref[...], block).astype(BF16)

            @pl.when(step + buffers < steps)
            def _():
                fetch(step + buffers).start()

            return carry

        lax.fori_loop(0, steps, body, 0)

    return pl.pallas_call(
        kernel,
        name=f"backward_rows_{part}",
        in_specs=[in_smem(), in_vmem(), in_place()],
        out_specs=in_vmem(),
        out_shape=shaped(seqs, count),
        scratch_shapes=[
            pltpu.VMEM((buffers, rows, dst_tile), BF16),
            pltpu.SemaphoreType.DMA((buffers,)),
        ],
        compiler_params=pltpu.CompilerParams(vmem_limit_bytes=24 * MIB),
        cost_estimate=cost(2 * seqs * count * dst_tile, 2 * count * dst_tile),
    )(place, message, transition)


def pair_sum(place, mine, theirs, groups):
    seqs = theirs.shape[0]
    width = theirs.shape[1] // groups

    def kernel(place_ref, *refs):
        parts, their_ref, slots = refs[: len(mine)], refs[len(mine)], refs[len(mine) + 1 : -1]
        whole = refs[-1]
        at = 0
        for part in parts:
            columns = slice(at, at + part.shape[1])
            whole[:, columns] = part[...].astype(F32) + their_ref[:, columns].astype(F32)
            at += part.shape[1]
        for r in range(groups):
            slots[r][...] = whole[:, span(lax.rem(place_ref[1] + r, groups), width)].astype(BF16)

    return pl.pallas_call(
        kernel,
        name="pair_sum",
        in_specs=[in_smem()] + [in_vmem()] * (len(mine) + 1),
        out_specs=[in_vmem()] * groups,
        out_shape=[shaped(seqs, width)] * groups,
        scratch_shapes=[pltpu.VMEM(theirs.shape, F32)],
        compiler_params=pltpu.CompilerParams(vmem_limit_bytes=6 * MIB),
        cost_estimate=cost(theirs.size, 8 * theirs.size),
    )(place, *mine, theirs)


def emission_sum(place, pieces, emit_cols, token_ids, position, inner_round):
    seqs, width = pieces[0].shape

    def kernel(place_ref, emit_ref, token_ref, *refs):
        summed = refs[0][...].astype(F32)
        for ref in refs[1:-1]:
            summed = summed + ref[...].astype(F32)
        if inner_round:
            summed = summed.astype(BF16).astype(F32)
        emission = emitted(token_ref, emit_ref, position, span(place_ref[0], width))
        refs[-1][...] = (scaling * emission * summed).astype(BF16)

    return pl.pallas_call(
        kernel,
        name=f"emission_sum_{position}",
        in_specs=[in_smem()] + [in_vmem()] * (2 + len(pieces)),
        out_specs=in_vmem(),
        out_shape=shaped(seqs, width),
        compiler_params=pltpu.CompilerParams(vmem_limit_bytes=6 * MIB),
        cost_estimate=cost(pieces[0].size, 8 * pieces[0].size),
    )(place, emit_cols, token_ids, *pieces)


def forward_quarter(place, own_slices, other_slices, transition, groups):
    seqs, width = own_slices[0].shape
    src_tile = transition.shape[0]
    dst_tile = transition.shape[1]
    wide = src_tile // 4
    piece = wide // groups

    def kernel(place_ref, *refs):
        slices, t_ref, slots = refs[: 2 * groups], refs[2 * groups], refs[2 * groups + 1 : 3 * groups + 1]
        total, held, sems = refs[3 * groups + 1 :]
        own, group, parity = place_ref[0], place_ref[1], place_ref[2]

        def fetch(step):
            row = step // groups * dst_tile + lax.rem(group - step % groups + groups, groups) * width
            row = pl.multiple_of(row, width)
            return pltpu.make_async_copy(
                t_ref.at[pl.ds(row, width), pl.ds(0, wide)], held.at[step], sems.at[step]
            )

        @pl.when(parity == 0)
        def _():
            for step in range(2 * groups):
                fetch(step).start()
            for step in range(2 * groups):
                fetch(step).wait()
                product = jnp.dot(slices[step][...], held[step], preferred_element_type=F32)
                if step == 0:
                    total[...] = product
                else:
                    total[...] += product
            for r in range(groups):
                slots[r][...] = total[:, span(lax.rem(own + r, groups), piece)].astype(BF16)

        @pl.when(parity != 0)
        def _():
            for r in range(groups):
                slots[r][...] = jnp.zeros_like(slots[r])

    return pl.pallas_call(
        kernel,
        name="forward_quarter",
        in_specs=[in_smem()] + [in_vmem()] * (2 * groups) + [in_place()],
        out_specs=[in_vmem()] * groups,
        out_shape=[shaped(seqs, piece)] * groups,
        scratch_shapes=[
            pltpu.VMEM((seqs, wide), F32),
            pltpu.VMEM((2 * groups, width, wide), BF16),
            pltpu.SemaphoreType.DMA((2 * groups,)),
        ],
        compiler_params=pltpu.CompilerParams(vmem_limit_bytes=40 * MIB),
        cost_estimate=cost(2 * seqs * src_tile * wide, 2 * src_tile * wide),
    )(place, *own_slices, *other_slices, transition)


def backward_quarter(place, slices, transition, groups):
    seqs, width = slices[0].shape
    dst_tile = transition.shape[1]
    quarter = dst_tile // 4
    rows = min(512, quarter)
    steps = quarter // rows

    def kernel(place_ref, *refs):
        parts, t_ref = refs[:groups], refs[groups]
        outs, whole_ref = refs[groups + 1 : groups + 3], refs[groups + 3]
        held, sems = refs[groups + 4 :]
        own, parity = place_ref[0], place_ref[2]

        def fetch(which, step):
            tile = 1 - parity if which == 0 else parity
            row = pl.multiple_of(tile * dst_tile + step * rows, rows)
            return pltpu.make_async_copy(
                t_ref.at[pl.ds(row, rows), :], held.at[which, step], sems.at[which, step]
            )

        for which in range(2):
            for step in range(steps):
                fetch(which, step).start()
        for r in range(groups):
            whole_ref[:, span(lax.rem(own - r + groups, groups), width)] = parts[r][...]
        for which in range(2):
            for step in range(steps):
                fetch(which, step).wait()
                product = rows_product(whole_ref[...], held[which, step])
                outs[which][:, step * rows : (step + 1) * rows] = product.astype(BF16)

    return pl.pallas_call(
        kernel,
        name="backward_quarter",
        in_specs=[in_smem()] + [in_vmem()] * groups + [in_place()],
        out_specs=[in_vmem()] * 3,
        out_shape=[shaped(seqs, quarter)] * 2 + [shaped(seqs, dst_tile)],
        scratch_shapes=[
            pltpu.VMEM((2, steps, rows, dst_tile), BF16),
            pltpu.SemaphoreType.DMA((2, steps)),
        ],
        compiler_params=pltpu.CompilerParams(vmem_limit_bytes=24 * MIB),
        cost_estimate=cost(4 * seqs * quarter * dst_tile, 4 * quarter * dst_tile),
    )(place, *slices, transition)


def expected_counts(place, own_slices, other_slices, two_slices, message_three, two_pieces, weights, transition, groups):
    seqs, width = own_slices[0].shape
    src_tile, dst_tile = transition.shape
    high, wide = src_tile // 4, dst_tile // 4
    rows = min(256, high)
    piece = high // groups
    narrow = wide // groups
    needed = high // width
    n_small = 4 * groups

    def kernel(place_ref, weight_ref, three_ref, t_ref, *refs):
        ones, twos, messages = refs[: 2 * groups], refs[2 * groups : 3 * groups], refs[3 * groups : n_small]
        out_ref, left, right = refs[n_small:]
        own, group, parity = place_ref[0], place_ref[1], place_ref[2]

        @pl.when(pl.program_id(0) == 0)
        def _():
            for r in range(groups):
                back = lax.rem(group - r + groups, groups)
                for which in range(2):

                    @pl.when((back < needed) & (parity == which))
                    def _():
                        left[:seqs, span(back, width)] = ones[which * groups + r][...]

                left[seqs:, span(back, piece)] = twos[r][...]
                back = lax.rem(own - r + groups, groups)
                scaled = weight_ref[...] * messages[r][...].astype(F32)
                right[:seqs, span(back, narrow)] = scaled.astype(BF16)
            right[seqs:, :] = (weight_ref[...] * three_ref[:, :wide].astype(F32)).astype(BF16)

        block = left[:, span(pl.program_id(0), rows)]
        outer = lax.dot_general(
            block, right[...], (((0,), (0,)), ((), ())), preferred_element_type=F32
        )
        out_ref[...] = t_ref[...].astype(F32) * outer

    return pl.pallas_call(
        kernel,
        name="expected_counts",
        grid=(high // rows,),
        in_specs=[in_smem(), in_vmem(), in_vmem(), pl.BlockSpec((rows, wide), lambda i: (i, 0))]
        + [in_vmem()] * n_small,
        out_specs=pl.BlockSpec((rows, wide), lambda i: (i, 0)),
        out_shape=shaped(high, wide, kind=F32),
        scratch_shapes=[pltpu.VMEM((2 * seqs, high), BF16), pltpu.VMEM((2 * seqs, wide), BF16)],
        compiler_params=pltpu.CompilerParams(vmem_limit_bytes=16 * MIB),
        cost_estimate=cost(4 * seqs * high * wide, 6 * high * wide),
    )(place, weights, message_three, transition, *own_slices, *other_slices, *two_slices, *two_pieces)


def per_device(transition, emit_cols, token_ids, alpha_start, beta_end, inverse_likelihood):
    groups = lax.axis_size("src")
    dst_count = lax.axis_size("dst")
    own = lax.axis_index("src")
    group = lax.axis_index("dst") // 2
    parity = lax.axis_index("dst") % 2
    place = jnp.stack([own, group, parity]).astype(jnp.int32)
    both = ("src", "dst")
    everywhere = [(s, g, k) for s in range(groups) for g in range(groups) for k in range(2)]

    def at(s, g, k):
        return s * dst_count + g * 2 + k

    def within(value, r, parities=(0, 1)):
        pairs = [(at(s, g, k), at((s + r) % groups, g, k)) for s, g, k in everywhere if k in parities]
        return lax.ppermute(value, both, pairs)

    def other_core(value, parities=(0, 1)):
        pairs = [(at(s, g, k), at(s, g, 1 - k)) for s, g, k in everywhere if k in parities]
        return lax.ppermute(value, both, pairs)

    def to_column(value, r, parities=(0, 1)):
        pairs = [(at(s, g, k), at(g, (s + r) % groups, k)) for s, g, k in everywhere if k in parities]
        return lax.ppermute(value, both, pairs)

    def to_plane(value, r):
        pairs = [(at(s, g, k), at((g + r) % groups, s, k)) for s, g, k in everywhere]
        return lax.ppermute(value, both, pairs)

    *slots, other_rows, message_four = first_pass(
        place, alpha_start, beta_end, emit_cols, token_ids, transition, groups
    )
    their_rows = other_core(other_rows)
    pieces = [slots[0]] + [within(slots[r], r) for r in range(1, groups)]
    mine = [backward_rows(place, message_four, transition, 0, 2)]
    one_slice = emission_sum(place, pieces, emit_cols, token_ids, 0, False)
    own_slices = [to_column(one_slice, r) for r in range(groups)]
    mine.append(backward_rows(place, message_four, transition, 1, 2))
    other_slices = [other_core(value) for value in own_slices]

    slots = pair_sum(place, mine, their_rows, groups)
    pieces = [to_plane(slots[r], r) for r in range(groups)]
    three_slice = emission_sum(place, pieces, emit_cols, token_ids, 2, True)
    slices = [three_slice] + [within(three_slice, r) for r in range(1, groups)]

    slots = forward_quarter(place, own_slices, other_slices, transition, groups)
    pieces = [slots[0]] + [within(slots[r], r, (0,)) for r in range(1, groups)]
    half_tile = emit_cols[:, : emit_cols.shape[1] // 2]
    two_slice = emission_sum(place, pieces, half_tile, token_ids, 1, False)
    two_slice = jnp.where(parity == 0, two_slice, other_core(two_slice, (0,)))
    two_slices = [to_column(two_slice, r) for r in range(groups)]

    other_rows, own_rows, message_three = backward_quarter(place, slices, transition, groups)
    their_rows = other_core(other_rows)
    slots = pair_sum(place, [own_rows], their_rows, groups)
    pieces = [to_plane(slots[r], r) for r in range(groups)]
    quarter_tile = emit_cols[:, : emit_cols.shape[1] // 4]
    two_piece = emission_sum(place, pieces, quarter_tile, token_ids, 1, True)
    two_pieces = [two_piece] + [within(two_piece, r) for r in range(1, groups)]

    return expected_counts(
        place,
        own_slices,
        other_slices,
        two_slices,
        message_three,
        two_pieces,
        inverse_likelihood[:, None],
        transition,
        groups,
    )


def solution(mesh):
    in_specs = (P("src", "dst"), P(None, "dst"), P(), P(None, "src"), P(None, "dst"), P())
    out_specs = P("src", "dst")
    groups, dst_count = mesh.shape["src"], mesh.shape["dst"]

    def whole(transition, *others):
        dst_tile = transition.shape[1] // dst_count
        aligned = dst_count == 2 * groups and groups % 2 == 0 and dst_tile % (4 * groups * 128) == 0
        return jax.shard_map(
            per_device if aligned else plain_device,
            mesh=mesh,
            in_specs=in_specs,
            out_specs=out_specs,
            check_vma=False,
        )(transition, *others)

    return whole
```
